256 devices in a mesh: energy: 64 (over z, x, core), sector: 4 (over y).
Axes of the slice: x: 4, y: 4, z: 8, core: 2. Of those that a mesh axis runs over, the one named last changes fastest.
Arguments:
- boundary: float32 [128, 2, 1024, 128], P('energy'), may hold values from -6 to 6
- energies: float32 [128], P('energy'), may hold values from 0.5 to 1.5
- levels: int32 [1024], replicated, may hold values from 0 to 31
- pattern: int32 [8, 8, 8], P('sector'), may hold values 0 or 1
- coupling: bfloat16 [8, 64, 128, 128], P('sector', 'energy'), may hold values from -0.125 to 0.125
Outputs:
- edge_state: float32 [4, 128, 2, 1024, 128], P('sector', 'energy')
The draws below stay inside these ranges and needn't reach their ends.
All inputs are finite; a program needn't handle non-finite values. No bound on the sum of `pattern` on one device may be relied on, other than what follows from the above.
Results may differ from the reference program's by a relative error of at most 0.0003.
Values may be sent and summed in bfloat16 or wider, within the bound.
No kernel may reach another device: no remote copies, remote signals or barrier semaphores. Data moves between devices by JAX's collectives and lax.ppermute only.
A program may use at most 64 MiB of HBM per device.

```python
import math
import jax
import jax.numpy as jnp
from jax import lax

BL = 128
NB = 8
NCOL = 128
SEC_DEV = 2
STEPS = 4
NCH = 1024
ENERGIES = 128
SECTORS = 8
N_SECTOR = 4


def touch_ends(array, stream_key, low, top_value):
    extent = array.shape
    spot = [jax.random.randint(jax.random.fold_in(stream_key, axis), (), 0, extent[axis]) for axis in range(len(extent))]
    array = array.at[tuple(spot)].set(low)
    longest = extent.index(max(extent))
    spot[longest] = (spot[longest] + 1) % extent[longest]
    return array.at[tuple(spot)].set(top_value)


def block_scale(key, dims, pieces, smallest, largest):
    gain, own = 1.0, jax.random.fold_in(key, 6)
    for position, blocks in pieces:
        steps = jnp.exp(jax.random.uniform(jax.random.fold_in(own, position), (blocks,), jnp.float32, smallest / len(pieces), largest / len(pieces)))
        gain = gain * jnp.repeat(steps, dims[position] // blocks).reshape([-1 if axis == position else 1 for axis in range(len(dims))])
    return gain


def normal_values(stream_key, extent, width, limit, split=(), kind=jnp.bfloat16):
    values = jax.random.normal(stream_key, extent, jnp.float32) * width
    if len(split) > 0:
        values = block_scale(stream_key, extent, split, -0.22, 0.18) * values
    return jnp.clip(values, min=-limit, max=limit).astype(kind)


def setup_inputs(seed: int = 0) -> dict:
    key_of = jax.random.split(jax.random.key(seed), 6)
    return {
        "boundary": normal_values(key_of[0], (ENERGIES, 2, NCH, NCOL), 1.0, 6.0, ((0, 64),), jnp.float32),
        "energies": jnp.clip(jnp.exp(math.log(1.5) - 1.0986123 * jax.random.uniform(key_of[1], (ENERGIES,), jnp.float32) ** block_scale(key_of[1], (ENERGIES,), ((0, 64),), -0.2, 0.2)), 0.5, 1.5),
        "levels": touch_ends(jax.random.randint(key_of[2], (NCH,), 0, 32), jax.random.fold_in(key_of[2], 1), 0, 31).astype(jnp.int32),
        "pattern": touch_ends((jax.random.randint(key_of[3], (SECTORS, NB, NB), 0, 2) < 1).astype(jnp.int32), jax.random.fold_in(key_of[3], 1), 0, 1),
        "coupling": normal_values(key_of[4], (SECTORS, NB * NB, BL, BL), (2 * NCH) ** -0.5, 0.125, ((0, 4), (1, 64))),
    }


def reference(boundary, energies, levels, pattern, coupling):
    step_len = 1.6 / (SECTORS * STEPS)
    shaped = coupling.reshape(SECTORS, NB, NB, BL, BL)
    diag_terms = 0.05 * levels.astype(jnp.float32)[None, :, None] - energies[:, None, None]
    field = boundary[:, 0]
    slope = boundary[:, 1]
    edges = []
    for run_index in range(N_SECTOR):
        for inner in range(SEC_DEV):
            sector = run_index * SEC_DEV + inner
            masked = shaped[sector] * pattern[sector].astype(jnp.bfloat16)[:, :, None, None]
            matrix = masked.astype(jnp.float32)
            for step in range(STEPS):
                low = field.astype(jnp.bfloat16)
                low = lax.optimization_barrier(low).astype(jnp.float32)
                low = low.reshape(ENERGIES, NB, BL, NCOL)
                coupled = jnp.einsum("ijab,ejbc->eiac", matrix, low).reshape(ENERGIES, NCH, NCOL)
                slope = slope + step_len * (diag_terms * field + coupled)
                field = field + step_len * slope
        edges.append(jnp.stack([field, slope], axis=1))
    return jnp.stack(edges, axis=0)
```

```python
import functools
import itertools

import jax
import jax.numpy as jnp
from jax import lax
from jax.experimental import pallas as pl
from jax.experimental.pallas import tpu as pltpu
from jax.sharding import Mesh
from jax.sharding import PartitionSpec as P

STEPS = 4
AXES = ("energy_0", "energy_1", "energy_2", "sector")
ENERGY = AXES[:3]


def moved(value, sizes, where_to):
    index = {place: at for at, place in enumerate(itertools.product(*map(range, sizes)))}
    pairs = []
    for place, at in index.items():
        target = where_to(*place)
        if target is not None:
            target = tuple(t % n for t, n in zip(target, sizes))
            pairs.append((at, index[target]))
    return lax.ppermute(value, AXES, pairs)


def core_swap(value, sizes):
    return moved(value, sizes, lambda z, x, c, y: (z, x, 1 - c, y))


def hop(value, sizes, axis):
    if axis == 0:
        return moved(value, sizes, lambda z, x, c, y: (z + 1 - 2 * c, x, c, y))
    return moved(value, sizes, lambda z, x, c, y: (z, x + 1 - 2 * c, c, y))


def first_ring(piece, sizes, axis, core):
    count = sizes[axis]
    rows = piece.shape[0] // 2
    got = [piece]
    for _ in range(count // 2 - 1):
        got.append(hop(got[-1], sizes, axis))
    half = hop(lax.dynamic_slice_in_dim(got[-1], core * rows, rows, 0), sizes, axis)
    mine = jnp.concatenate(got[1:] + [half], axis=0)
    other = core_swap(mine, sizes)
    full = piece.shape[0]
    others = [other[i * full : (i + 1) * full] for i in range(count // 2 - 1)]
    other_half = other[(count // 2 - 1) * full :]
    middle = jnp.where(
        core == 0,
        jnp.concatenate([half, other_half], axis=0),
        jnp.concatenate([other_half, half], axis=0),
    )
    return jnp.stack(got + [middle] + others[::-1], axis=0)


def second_ring(tiles, sizes, axis, core):
    count = sizes[axis]
    rows = tiles.shape[0] // 2
    out = [(tiles, 0, "own")]
    now = tiles
    for r in range(1, count // 2):
        now = hop(now, sizes, axis)
        out.append((now, r, "own"))
        out.append((core_swap(now, sizes), r, "other"))
    half = hop(lax.dynamic_slice_in_dim(now, core, rows, 0), sizes, axis)
    out.append((half, count // 2, "own_half"))
    out.append((core_swap(half, sizes), count // 2, "other_half"))
    return out


def places(kind, rounds, j, core):
    if kind == "own":
        return j, rounds
    if kind == "other":
        return -j, -rounds
    if kind == "own_half":
        return j + core, rounds
    return -(j + 1 - core), rounds


def run_kernel(layout, pick, back, step_len, sizes, *refs):
    n_in = len(layout)
    pieces = refs[:n_in]
    state_ref, hq_ref, out_ref, v_ref, low_ref, sems = refs[n_in:]
    z, x, core, y = (lax.axis_index(name) for name in AXES)
    sign = 1 - 2 * core
    channels = v_ref.shape[1]
    tile_rows, tile_cols = pieces[0].shape[2], pieces[0].shape[3]
    rows = 256
    active = y >= back

    @pl.when(active)
    def _():
        for (first_axis, kind, rounds), ref in zip(layout, pieces):
            part = 0 if first_axis == 0 else 1
            for j in range(ref.shape[0]):
                a, b = places(kind, rounds, j, core)
                if first_axis == 0:
                    zz, xx = z - sign * a, x - sign * b
                else:
                    zz, xx = z - sign * b, x - sign * a
                zz = lax.rem(zz + 2 * sizes[0], sizes[0])
                xx = lax.rem(xx + 3 * sizes[1], sizes[1])
                pltpu.make_async_copy(
                    ref.at[j, pick],
                    v_ref.at[
                        part,
                        pl.ds(pl.multiple_of(zz * tile_rows, tile_rows), tile_rows),
                        pl.ds(pl.multiple_of(xx * tile_cols, tile_cols), tile_cols),
                    ],
                    sems.at[part],
                ).start()

    out_ref[...] = state_ref[...]

    @pl.when(active)
    def _():
        for e in range(2):
            low_ref[0, :, e * 128 : (e + 1) * 128] = state_ref[e, 0].astype(jnp.bfloat16)

        def step(part, now):
            low = low_ref[now]
            for i in range(channels // rows):
                r = slice(i * rows, (i + 1) * rows)
                coupled = jnp.dot(v_ref[part, r, :], low, preferred_element_type=jnp.float32)
                for e in range(2):
                    cols = slice(e * 128, (e + 1) * 128)
                    field = out_ref[e, 0, r, :]
                    slope = out_ref[e, 1, r, :] + (
                        hq_ref[r, cols] * field + step_len * coupled[:, cols]
                    )
                    field = field + step_len * slope
                    out_ref[e, 1, r, :] = slope
                    out_ref[e, 0, r, :] = field
                    low_ref[1 - now, r, cols] = field.astype(jnp.bfloat16)

        for part in range(2):
            pltpu.make_async_copy(v_ref.at[part], v_ref.at[part], sems.at[part]).wait()

            def two(_, carry):
                step(part, 0)
                step(part, 1)
                return carry

            lax.fori_loop(0, STEPS // 2, two, 0)


def run_call(pieces, layout, pick, back, step_len, sizes, state, hq):
    channels = state.shape[2]
    return pl.pallas_call(
        functools.partial(run_kernel, layout, pick, back, step_len, sizes),
        out_shape=jax.ShapeDtypeStruct(state.shape, jnp.float32),
        in_specs=[pl.BlockSpec(memory_space=pl.ANY)] * len(pieces)
        + [pl.BlockSpec(memory_space=pltpu.VMEM)] * 2,
        out_specs=pl.BlockSpec(memory_space=pltpu.VMEM),
        scratch_shapes=[
            pltpu.VMEM((2, channels, channels), jnp.bfloat16),
            pltpu.VMEM((2, channels, 256), jnp.bfloat16),
            pltpu.SemaphoreType.DMA((2,)),
        ],
        compiler_params=pltpu.CompilerParams(vmem_limit_bytes=20 << 20),
        cost_estimate=pl.CostEstimate(
            flops=4 * STEPS * channels * channels * 256, bytes_accessed=8 << 20, transcendentals=0
        ),
    )(*pieces, state, hq)


def body(sizes, boundary, energies, levels, pattern, coupling):
    z, x, core, y = (lax.axis_index(name) for name in AXES)
    n_run = sizes[3]
    sec_dev = coupling.shape[0]
    step_len = 1.6 / (sec_dev * STEPS * n_run)
    place = (z * sizes[1] + x) * sizes[2] + core
    side = pattern.shape[1]
    present = lax.dynamic_slice(
        pattern, (0, place // side, place % side), (sec_dev, 1, 1)
    ).astype(jnp.bfloat16)
    shard = coupling[:, 0] * present
    behind = [shard]
    for k in range(1, n_run):
        behind.append(
            moved(shard, sizes, lambda z, x, c, y: (z, x, c, y + k) if y + k < n_run else None)
        )
    thresholds = 0.05 * levels.astype(jnp.float32)
    hq = step_len * (thresholds[:, None] - jnp.repeat(energies, boundary.shape[3])[None, :])

    waves = [(3, 2), (1, 0)]
    state = boundary
    for wave in waves:
        mine = jnp.stack([behind[k] for k in wave], axis=0)
        other = core_swap(mine, sizes)
        both = jnp.where(
            core == 0,
            jnp.concatenate([mine, other], axis=-1),
            jnp.concatenate([other, mine], axis=-1),
        )
        layout, pieces = [], []
        for first, second, parity in ((0, 1, 0), (1, 0, 1)):
            tiles = first_ring(both[:, parity], sizes, first, core)
            for array, rounds, kind in second_ring(tiles, sizes, second, core):
                layout.append((first, kind, rounds))
                pieces.append(array)
        for pick, back in enumerate(wave):
            state = run_call(pieces, layout, pick, back, step_len, sizes, state, hq)
    return state[None]


def solution(mesh):
    sizes = (8, 4, 2, mesh.shape["sector"])
    split = Mesh(mesh.devices.reshape(sizes), AXES)
    placed = (
        P(ENERGY, None, None, None),
        P(ENERGY),
        P(),
        P("sector", None, None),
        P("sector", ENERGY, None, None),
    )
    return jax.shard_map(
        functools.partial(body, sizes),
        mesh=split,
        in_specs=placed,
        out_specs=P("sector", ENERGY, None, None, None),
        check_vma=False,
    )
```

```python
import functools
import itertools

import jax
import jax.numpy as jnp
from jax import lax
from jax.experimental import pallas as pl
from jax.experimental.pallas import tpu as pltpu
from jax.sharding import Mesh
from jax.sharding import PartitionSpec as P

STEPS = 4
WAVES = ((3, 2, 1, 0),)
AXES = ("energy_0", "energy_1", "energy_2", "sector")
ENERGY = AXES[:3]


def moved(value, sizes, where_to):
    index = {place: at for at, place in enumerate(itertools.product(*map(range, sizes)))}
    pairs = []
    for place, at in index.items():
        target = where_to(*place)
        if target is not None:
            target = tuple(t % n for t, n in zip(target, sizes))
            pairs.append((at, index[target]))
    return lax.ppermute(value, AXES, pairs)


def core_swap(value, sizes):
    return moved(value, sizes, lambda z, x, c, y: (z, x, 1 - c, y))


TILE_Z = (0, -1, -2, -3, 1, 2, 3, 4)
SLAB_X = (0, -1, 1, 2)


def by_core(core, zero, one):
    return jnp.where(core == 0, zero, one)


def ends(core, mine, other):
    return by_core(core, mine, other), by_core(core, other, mine)


def pack_kernel(plans, n_in, *refs):
    core = lax.axis_index(AXES[2])
    sources, outs = refs[:n_in], refs[n_in:]

    def copy(side, both):
        for out, plan in zip(outs, plans):
            for t, choice in enumerate(plan):
                if (choice[0] == choice[1]) == both:
                    source, i = choice[side]
                    out[t] = sources[source][i]

    copy(0, True)
    for side in range(2):
        pl.when(core == side)(functools.partial(copy, side, False))


def pack(plans, *sources):
    tile = sources[0].shape[1:]
    return pl.pallas_call(
        functools.partial(pack_kernel, plans, len(sources)),
        out_shape=[jax.ShapeDtypeStruct((len(plan), *tile), sources[0].dtype) for plan in plans],
        in_specs=[pl.BlockSpec(memory_space=pltpu.VMEM)] * len(sources),
        out_specs=[pl.BlockSpec(memory_space=pltpu.VMEM)] * len(plans),
        compiler_params=pltpu.CompilerParams(vmem_limit_bytes=16 << 20),
    )(*sources)


def same(source, tiles):
    return [((source, t), (source, t)) for t in tiles]


def entries(kinds, z, x, core):
    for kind, whose, ks, ref in kinds:
        side = core if whose == "mine" else 1 - core
        sign = 1 - 2 * side
        if kind[0] == "x":
            half = side if kind[1] != "b" else 1 - side
            dx = {"own": 0, "one": -sign, "two": 2}[kind[2:]]
            yield 0, ref, [
                ((len(TILE_Z) // 2 * i + j,), k, z + by_core(half, TILE_Z[j], TILE_Z[4 + j]), x + dx)
                for i, k in enumerate(ks)
                for j in range(4)
            ]
        else:
            half = side if kind[1] != "b" else 1 - side
            k = {"own": 0, "one": 1 + 2 * side, "two": 2}[kind[2:]]
            yield 1, ref, [
                ((len(TILE_Z) * i + j,), k, z + dz, x + by_core(half, SLAB_X[i], SLAB_X[2 + i]))
                for i in range(2)
                for j, dz in enumerate(TILE_Z)
            ]


def wave_kernel(kinds, n_run, step_len, sizes, *refs):
    n_in = len(kinds)
    pieces = refs[:n_in]
    state_ref, hq_ref, out_ref, v_ref, low_ref, sems = refs[n_in:]
    z, x, core, y = (lax.axis_index(name) for name in AXES)
    channels = v_ref.shape[1]
    tile_rows, tile_cols = pieces[0].shape[1], pieces[0].shape[2]
    rows = 256

    for part, ref, tiles in entries([(*kind, ref) for kind, ref in zip(kinds, pieces)], z, x, core):
        groups = {}
        for tile in tiles:
            groups.setdefault(id(tile[1]), (tile[1], []))[1].append(tile)

        for k, group in groups.values():

            @pl.when(y >= k)
            def _(k=k, group=group, part=part, ref=ref):
                slot = 2 * (n_run - 1 - k) + part
                for index, _, zz, xx in group:
                    zz = lax.rem(zz + sizes[0], sizes[0])
                    xx = lax.rem(xx + sizes[1], sizes[1])
                    pltpu.make_async_copy(
                        ref.at[index],
                        v_ref.at[
                            slot,
                            pl.ds(pl.multiple_of(zz * tile_rows, tile_rows), tile_rows),
                            pl.ds(pl.multiple_of(xx * tile_cols, tile_cols), tile_cols),
                        ],
                        sems.at[slot],
                    ).start()

    out_ref[...] = state_ref[...]
    for e in range(2):
        low_ref[0, :, e * 128 : (e + 1) * 128] = state_ref[e, 0].astype(jnp.bfloat16)

    def step(slot, now):
        low = low_ref[now]
        for i in range(channels // rows):
            r = slice(i * rows, (i + 1) * rows)
            coupled = jnp.dot(v_ref[slot, r, :], low, preferred_element_type=jnp.float32)
            for e in range(2):
                cols = slice(e * 128, (e + 1) * 128)
                field = out_ref[e, 0, r, :]
                slope = out_ref[e, 1, r, :] + (
                    hq_ref[r, cols] * field + step_len * coupled[:, cols]
                )
                field = field + step_len * slope
                out_ref[e, 1, r, :] = slope
                out_ref[e, 0, r, :] = field
                low_ref[1 - now, r, cols] = field.astype(jnp.bfloat16)

    def sector(slot, carry):
        pltpu.make_async_copy(v_ref.at[slot], v_ref.at[slot], sems.at[slot]).wait()
        for s in range(STEPS):
            step(slot, s % 2)
        return carry

    lax.fori_loop(2 * (n_run - 1 - y), 2 * n_run, sector, 0)


def wave_call(pieces, kinds, n_run, step_len, sizes, state, hq):
    channels = state.shape[2]
    return pl.pallas_call(
        functools.partial(wave_kernel, kinds, n_run, step_len, sizes),
        out_shape=jax.ShapeDtypeStruct(state.shape, jnp.float32),
        in_specs=[pl.BlockSpec(memory_space=pl.ANY)] * len(pieces)
        + [pl.BlockSpec(memory_space=pltpu.VMEM)] * 2,
        out_specs=pl.BlockSpec(memory_space=pltpu.VMEM),
        scratch_shapes=[
            pltpu.VMEM((2 * n_run, channels, channels), jnp.bfloat16),
            pltpu.VMEM((2, channels, 256), jnp.bfloat16),
            pltpu.SemaphoreType.DMA((2 * n_run,)),
        ],
        compiler_params=pltpu.CompilerParams(vmem_limit_bytes=26 << 20),
        cost_estimate=pl.CostEstimate(
            flops=4 * n_run * STEPS * channels * channels * 256,
            bytes_accessed=16 << 20,
            transcendentals=0,
        ),
    )(*pieces, state, hq)


def body(sizes, boundary, energies, levels, pattern, coupling):
    z, x, core, y = (lax.axis_index(name) for name in AXES)
    n_run = sizes[3]
    sec_dev = coupling.shape[0]
    step_len = 1.6 / (sec_dev * STEPS * n_run)
    place = (z * sizes[1] + x) * sizes[2] + core
    side = pattern.shape[1]
    present = lax.dynamic_slice(
        pattern, (0, place // side, place % side), (sec_dev, 1, 1)
    ).astype(jnp.bfloat16)
    shard = coupling[:, 0] * present
    thresholds = 0.05 * levels.astype(jnp.float32)
    hq = step_len * (thresholds[:, None] - jnp.repeat(energies, boundary.shape[3])[None, :])
    send = functools.partial(moved, sizes=sizes)
    swap = functools.partial(core_swap, sizes=sizes)

    chip = jnp.concatenate(ends(core, shard, swap(shard)), axis=-1)

    got = [
        send(chip, where_to=lambda z, x, c, y, d=d: (z + (1 - 2 * c) * d, x, c, y)) for d in (1, 2, 3)
    ]
    far = send(
        lax.dynamic_slice_in_dim(chip, core, 1, 0), where_to=lambda z, x, c, y: (z + 4, x, c, y)
    )
    (mine,) = pack([same(0, (0, 1)) + same(1, (0, 1)) + same(2, (0, 1)) + same(3, (0,))], *got, far)
    other = swap(mine)

    def tiles_of(s):
        low = [((1, 2 * i + s), (2, 2 * i + s)) for i in range(3)]
        high = [((2, 2 * i + s), (1, 2 * i + s)) for i in range(3)]
        last = ((1 + s, 6), (2 - s, 6))
        return same(0, (s,)) + low + high + [last]

    def halves(plan):
        return [(plan[t][0], plan[4 + t][1]) for t in range(4)]

    plans = [tiles_of(0), tiles_of(1)]
    x_tiles, y_tiles, x_half, y_half = pack(plans + [halves(p) for p in plans], chip, mine, other)

    def x_near(z, x, c, y):
        if c == 0:
            return (z, x, c, y + 1) if y < n_run - 1 else None
        return (z, x, c, y - 1) if y == 0 else None

    x_one = send(x_tiles, where_to=x_near)
    y_one = send(y_tiles, where_to=lambda z, x, c, y: (z, x + 1 - 2 * c, c, y))
    x_two = send(x_half, where_to=lambda z, x, c, y: (z, x, c, y + 2) if y < n_run - 2 else None)
    y_two = send(y_half, where_to=lambda z, x, c, y: (z, x + 2, c, y))
    x_one, y_one, x_two, y_two = lax.optimization_barrier((x_one, y_one, x_two, y_two))
    (mine,) = pack([same(0, range(8)) + same(1, range(4)) + same(2, range(8)) + same(3, range(4))], x_one, x_two, y_one, y_two)
    other = swap(mine)

    def got_by(side, tiles):
        return [((2 + side, t), (3 - side, t)) for t in tiles]

    runs = {
        3: got_by(1, range(8)),
        2: got_by(0, range(8, 12)) + got_by(1, range(8, 12)),
        1: got_by(0, range(8)),
        0: same(0, range(8)),
    }
    slabs = [
        same(1, range(8)),
        got_by(0, range(12, 20)),
        got_by(1, range(12, 20)),
        got_by(0, range(20, 24)) + got_by(1, range(20, 24)),
    ]

    def split(low, high):
        return [[(p[0], q[1]) for p, q in zip(a, b)] for a, b in ((low, high), (high, low))]

    waves = WAVES
    plans = []
    for ks in waves:
        plans += split(sum((runs[k][:4] for k in ks), []), sum((runs[k][4:] for k in ks), []))
    plans += split(slabs[0] + slabs[1], slabs[2] + slabs[3])
    packed = pack(plans, x_tiles, y_tiles, mine, other)

    def x_hop(z, x, c, y):
        return (z, x + 1 - 2 * c, c, y)

    def y_hop(up, down):
        def where_to(z, x, c, y):
            return (z, x, c, y + 1 - 2 * c) if y in (down if c else up) else None

        return where_to

    pieces, kinds = [], []

    def keep(array, kind, ks, gate=None):
        pieces.append(array)
        kinds.append((kind, "mine", ks))
        if kind[2:] != "own":
            if gate is not None:
                array, gate = lax.optimization_barrier((array, gate))
            pieces.append(swap(array))
            kinds.append((kind, "other", ks))
        return pieces[-1]

    def stream(name, ks, a, b, hops):
        keep(a, name + "aown", ks)
        keep(b, name + "bown", ks)
        a_one = send(a, where_to=hops[0])
        b_one = send(b, where_to=hops[1])
        a_two = send(a_one, where_to=hops[2])
        gate = keep(a_one, name + "aone", ks)
        gate = keep(b_one, name + "bone", ks, gate)
        keep(a_two, name + "atwo", ks, gate)

    y_hops = (y_hop((0, 1, 2), (0, 1)), y_hop((0, 1, 2), (0,)), y_hop((1, 2), (0, 3)))
    for w, ks in enumerate(waves):
        stream("x", ks, packed[2 * w], packed[2 * w + 1], (x_hop,) * 3)
    stream("y", (), packed[-2], packed[-1], y_hops)
    state = wave_call(pieces, kinds, n_run, step_len, sizes, boundary, hq)
    return state[None]


def solution(mesh):
    sizes = (8, 4, 2, mesh.shape["sector"])
    split = Mesh(mesh.devices.reshape(sizes), AXES)
    placed = (
        P(ENERGY, None, None, None),
        P(ENERGY),
        P(),
        P("sector", None, None),
        P("sector", ENERGY, None, None),
    )
    return jax.shard_map(
        functools.partial(body, sizes),
        mesh=split,
        in_specs=placed,
        out_specs=P("sector", ENERGY, None, None, None),
        check_vma=False,
    )
```
